512 devices in a mesh: dom: 32 (over z, core), head: 16 (over x, y).
Axes of the slice: x: 4, y: 4, z: 16, core: 2. Of those that a mesh axis runs over, the one named last changes fastest.
Arguments:
- features: bfloat16 [262144, 512], P(('dom', 'head')), may hold values from -16 to 16
- tile_pattern: int32 [2048, 6, 128, 128], P(('dom', 'head')), may hold values 0 or 1
- tile_source: int32 [2048, 6], P(('dom', 'head')), may hold values from 0 to 35
- serve_list: int32 [32, 16, 32, 1], P('dom', 'head'), may hold values from 0 to 3
- key_blocks: int32 [2048, 8], P('dom'), may hold values from 0 to 63, all different within a row
- qkv_weight: bfloat16 [512, 1536], replicated, may hold values from -0.25 to 0.25
- attn_weight: bfloat16 [512, 512], replicated, may hold values from -0.25 to 0.25
- norm_gain: float32 [512], replicated, may hold values from 0.5 to 1.5
- expand_weight: bfloat16 [2048, 512], P('head'), may hold values from -0.25 to 0.25
- reduce_weight: bfloat16 [2048, 512], P('head'), may hold values from -0.125 to 0.125
Outputs:
- output: bfloat16 [262144, 512], P(('dom', 'head'))
The draws below stay inside these ranges and needn't reach their ends.
Inputs may be any that keep to these rules, and one draw needn't show every extreme that they name: `key_blocks`: the 8 entries of a row are distinct.
All inputs are finite; a program needn't handle non-finite values. No bound on the sum of `tile_pattern` on one device may be relied on, other than what follows from the above.
Results may differ from the reference program's by a relative error of at most 0.01.
The reference program's roundings to bfloat16 on the way (of `aggregated`, `qkv`, `probabilities`, `context`, `normed` and `hidden`) count: a program that leaves them out, or rounds other values in their place, can miss the bound.
Values may be sent and summed in bfloat16 or wider, within the bound.
No kernel may reach another device: no remote copies, remote signals or barrier semaphores. Data moves between devices by JAX's collectives and lax.ppermute only.
A program may use at most 128 MiB of HBM per device.

```python
import jax
import jax.numpy as jnp
from jax import lax

D = 512
HEADS = 16
FF = 2048
HDIM = 32
BLOCK = 128
TPB = 6
SLOTS = 1
BLK_DEV = 4
BLK_PART = 64
KB = 8
NBLK = 2048
NODES = 262144
N_DOM = 32
N_HEAD = 16


def draw_features(key, part):
    key_base = jax.random.fold_in(jax.random.fold_in(key, 11), 0)
    values = jax.random.normal(key_base, (NODES, D), jnp.float32)
    return jnp.clip(values, -16.0, 16.0).astype(jnp.bfloat16)


def place_ends(drawn, key, low, largest):
    place = [jax.random.randint(jax.random.fold_in(key, axis), (), 0, length) for axis, length in enumerate(drawn.shape)]
    main_axis = drawn.shape.index(max(drawn.shape))
    neighbour = place[:main_axis] + [(place[main_axis] + 1) % drawn.shape[main_axis]] + place[main_axis + 1:]
    return drawn.at[tuple(place)].set(low).at[tuple(neighbour)].set(largest)


def block_levels(own_key, extent, pieces, least, high):
    def one(dim, shards_of):
        steps = jax.random.uniform(jax.random.fold_in(jax.random.fold_in(own_key, 6), dim), (shards_of,), jnp.float32, least / len(pieces), high / len(pieces))
        return jnp.repeat(jnp.exp(steps), extent[dim] // shards_of).reshape((-1,) + (1,) * (len(extent) - dim - 1))

    gain = one(*pieces[0])
    for cut in pieces[1:]:
        gain = gain * one(*cut)
    return gain


def different_ones(key, rows, count, top, lift):
    ranking = jax.random.permutation(jax.random.fold_in(key, 1), count)
    favour = ranking
    for power in range(3):
        favour = favour * favour // count
    favour = favour * lift // count
    lots = jax.random.randint(jax.random.fold_in(key, 2), (rows, count), 0, 4096) + favour
    fixed_rows = jax.random.permutation(jax.random.fold_in(key, 3), rows)[jnp.arange(count) % rows]
    lots = jnp.where(jnp.arange(rows)[:, None] == fixed_rows[None, :], 1 << 14, lots)
    merit = lots * count + jnp.arange(count)
    return lax.top_k(merit.astype(jnp.int32), top)[1].astype(jnp.int32)


def noise(own_key, shape, deviation, bound, cuts=(), held_as=jnp.bfloat16):
    level = block_levels(own_key, shape, cuts, -0.22, 0.18) if cuts else 1.0
    array = jax.random.normal(own_key, shape, jnp.float32) * deviation * level
    return jnp.minimum(jnp.maximum(array, -bound), bound).astype(held_as)


def setup_inputs(seed: int = 0) -> dict:
    seeds = jax.random.split(jax.random.key(seed), 11)
    features = draw_features(jax.random.fold_in(seeds[10], 71), 0)
    tile_pattern = place_ends((jax.random.randint(seeds[1], (NBLK, TPB, BLOCK, BLOCK), 0, 4) < 1).astype(jnp.int32), jax.random.fold_in(seeds[1], 1), 0, 1)
    tile_source = place_ends(jax.random.randint(seeds[2], (NBLK, TPB), 0, BLK_DEV + N_DOM * SLOTS), jax.random.fold_in(seeds[2], 1), 0, (BLK_DEV + N_DOM * SLOTS) - 1).astype(jnp.int32)
    serve_list = place_ends(jax.random.randint(seeds[3], (N_DOM, N_HEAD, N_DOM, SLOTS), 0, BLK_DEV), jax.random.fold_in(seeds[3], 1), 0, BLK_DEV - 1).astype(jnp.int32)
    key_blocks = different_ones(seeds[4], NBLK, BLK_PART, KB, 0)
    qkv_weight = noise(seeds[5], (D, 3 * D), D ** -0.5, 0.25)
    attn_weight = noise(seeds[6], (D, D), D ** -0.5, 0.25)
    norm_gain = jnp.clip(1.0 + 0.1 * jax.random.normal(seeds[7], (D,), jnp.float32), 0.5, 1.5)
    expand_weight = noise(seeds[8], (FF, D), D ** -0.5, 0.25, ((0, 16),))
    reduce_weight = noise(seeds[9], (FF, D), FF ** -0.5, 0.125, ((0, 16),))
    return dict(features=features, tile_pattern=tile_pattern, tile_source=tile_source, serve_list=serve_list, key_blocks=key_blocks, qkv_weight=qkv_weight, attn_weight=attn_weight, norm_gain=norm_gain, expand_weight=expand_weight, reduce_weight=reduce_weight)


def reference(features, tile_pattern, tile_source, serve_list, key_blocks, qkv_weight, attn_weight, norm_gain, expand_weight, reduce_weight):
    block_count = features.shape[0] // BLOCK
    blocks = features.reshape(block_count, BLOCK, D)
    block_ids = jnp.arange(block_count, dtype=jnp.int32)
    device_id = block_ids // BLK_DEV
    domain = (device_id // N_HEAD)[:, None]
    head_slot = (device_id % N_HEAD)[:, None]
    entries = tile_source
    remote_entry = jnp.maximum(entries - BLK_DEV, 0)
    peer_domain = remote_entry // SLOTS
    slot_index = remote_entry % SLOTS
    local_index = serve_list[peer_domain, head_slot, domain, slot_index]
    remote_block = (peer_domain * N_HEAD + head_slot) * BLK_DEV + local_index
    own_block = device_id[:, None] * BLK_DEV + entries
    source_block = jnp.where(entries < BLK_DEV, own_block, remote_block).astype(jnp.int32)

    def one_block(inputs):
        pattern_block, source_ids, own_rows = inputs
        sources = blocks[source_ids]
        summed = jnp.einsum('tij,tjf->if', pattern_block.astype(jnp.float32), sources.astype(jnp.float32))
        degree = lax.optimization_barrier(jnp.sum(pattern_block, axis=(0, 2))).astype(jnp.float32)
        return ((own_rows.astype(jnp.float32) + summed) * lax.rsqrt(1.0 + degree)[:, None]).astype(jnp.bfloat16)
    aggregated = lax.map(one_block, (tile_pattern, source_block, blocks)).reshape(-1, D)
    qkv = jnp.dot(aggregated, qkv_weight, preferred_element_type=jnp.float32).astype(jnp.bfloat16)
    qkv_parts = qkv.reshape(N_DOM, BLK_PART, BLOCK, HEADS, 3, HDIM)
    key_parts = key_blocks.reshape(N_DOM, BLK_PART, KB)
    score_scale = 1.0 / HDIM ** 0.5

    def one_part(inputs):
        part_qkv, part_keys = inputs

        def one_query(query_index):
            queries = part_qkv[query_index][:, :, 0, :].astype(jnp.float32)
            selected = part_qkv[part_keys[query_index]]
            keys = selected[:, :, :, 1, :].reshape(KB * BLOCK, HEADS, HDIM).astype(jnp.float32)
            values = selected[:, :, :, 2, :].reshape(KB * BLOCK, HEADS, HDIM).astype(jnp.float32)
            scores = jnp.einsum('qhe,khe->hqk', queries, keys) * score_scale
            row_max = lax.optimization_barrier(jnp.max(scores, axis=-1, keepdims=True))
            exp_terms = jnp.exp(scores - row_max)
            probabilities = (exp_terms / lax.optimization_barrier(jnp.sum(exp_terms, axis=-1, keepdims=True))).astype(jnp.bfloat16)
            context = jnp.einsum('hqk,khe->qhe', probabilities.astype(jnp.float32), values)
            return context.astype(jnp.bfloat16)
        return lax.map(one_query, jnp.arange(BLK_PART, dtype=jnp.int32))
    context = lax.map(one_part, (qkv_parts, key_parts)).reshape(-1, D)
    mixed = aggregated.astype(jnp.float32) + jnp.dot(context, attn_weight, preferred_element_type=jnp.float32)
    mean_square = lax.optimization_barrier(jnp.mean(mixed * mixed, axis=-1, keepdims=True))
    normed = (mixed * lax.rsqrt(mean_square + 1e-06) * norm_gain).astype(jnp.bfloat16)
    expanded = jnp.dot(normed, expand_weight.T, preferred_element_type=jnp.float32)
    hidden = jax.nn.gelu(expanded).astype(jnp.bfloat16)
    result = normed.astype(jnp.float32) + jnp.dot(hidden, reduce_weight, preferred_element_type=jnp.float32)
    return result.astype(jnp.bfloat16)
```

```python
import functools
import math

import jax
import jax.numpy as jnp
from jax import lax
from jax.experimental import pallas as pl
from jax.experimental.pallas import tpu as pltpu
from jax.sharding import PartitionSpec as P

HEADS = 16
HDIM = 32
BLOCK = 128
VM = pl.BlockSpec(memory_space=pltpu.VMEM)
SM = pl.BlockSpec(memory_space=pltpu.SMEM)
ANY = pl.BlockSpec(memory_space=pl.ANY)
EXP2_SCALE = math.log2(math.e) / math.sqrt(HDIM)


def ring_pieces(x, sides):
    tied = {}
    n = lax.axis_size("dom")
    half = n // 4
    cut = x.shape[0] // 2

    def send(v, by):
        return lax.ppermute(v, "dom", [(i, (i + by) % n) for i in range(n)])

    def trade(v):
        return lax.ppermute(v, "dom", [(i, i ^ 1) for i in range(n)])

    up, down = [x], [x]
    up_t, down_t = [trade(x)], []
    for k in range(1, half + 1):
        u_in, d_in = up[-1], down[-1]
        if k in sides:
            u_in, tied[k] = lax.optimization_barrier((u_in, sides[k]))
        if k == half:
            u_in, d_in = u_in[:cut], d_in[cut:]
        if k >= 3:
            u_in, down_t[-1] = lax.optimization_barrier((u_in, down_t[-1]))
        up.append(send(u_in, 2))
        if k >= 3:
            d_in, up_t[-1] = lax.optimization_barrier((d_in, up_t[-1]))
        down.append(send(d_in, -2))
        up_t.append(trade(up[-1]))
        down_t.append(trade(down[-1]))
    whole = up[:half] + down[1:half] + up_t[:half] + down_t[: half - 1]
    return whole + [up[half], down[half], up_t[half], down_t[half - 1]], tied


def piece_sources(n):
    d = lax.axis_index("dom")
    core = d % 2
    z, chips = d // 2, n // 2
    half = n // 4
    k = jnp.arange(half + 1)
    up = 2 * ((z - k) % chips) + core
    down = 2 * ((z + k) % chips) + core
    near = jnp.concatenate([up[:half], down[1:half]])
    flip = 1 - 2 * core
    return jnp.concatenate([near, near + flip, up[half:], up[half:] + flip]).astype(jnp.int32)


def piece_of_source(p, n):
    d = lax.axis_index("dom")
    core = d % 2
    z, chips = d // 2, n // 2
    half = n // 4
    k = (z - p // 2) % chips
    other = jnp.where((p % 2) == core, 0, 1)
    near = jnp.where(k < half, k, half - 1 + chips - k)
    return jnp.where(k == half, 2 * (2 * half - 1) + other, near + other * (2 * half - 1))


def aggregate_kernel(slot_ref, serve_ref, pattern_ref, own_ref, wt_ref, *rest):
    pieces, (agg_ref, qkv_ref, table, sems) = rest[:-4], rest[-4:]
    blocks, tiles = pattern_ref.shape[0], pattern_ref.shape[1]
    whole, halves = pieces[:-4], pieces[-4:]
    copies = []

    def copy_of(i, piece, block):
        start = pl.multiple_of(block * BLOCK, BLOCK)
        return pltpu.make_async_copy(
            piece.at[pl.ds(start, BLOCK), :], table.at[blocks + i], sems.at[i]
        )

    for i, piece in enumerate(whole):
        copies.append(copy_of(i, piece, serve_ref[i]))
        copies[-1].start()
    for i in range(2):
        slot, first = len(whole) + i, blocks // 2
        block = serve_ref[slot]

        @pl.when(block < first)
        def _(slot=slot, piece=halves[2 * i], block=block):
            copy_of(slot, piece, block).start()

        @pl.when(block >= first)
        def _(slot=slot, piece=halves[2 * i + 1], block=block - first):
            copy_of(slot, piece, block).start()

        copies.append(copy_of(slot, halves[2 * i], 0))
    for b in range(blocks):
        table[b] = own_ref[b * BLOCK : (b + 1) * BLOCK, :]
    for copy in copies:
        copy.wait()

    def one_block(b, carry):
        acc = table[b].astype(jnp.float32)
        count = jnp.zeros((BLOCK, BLOCK), jnp.int32)
        for t in range(tiles):
            pattern = pattern_ref[b, t]
            count = count + pattern
            acc = acc + jnp.dot(
                pattern.astype(jnp.float32).astype(jnp.bfloat16),
                table[slot_ref[b * tiles + t]],
                preferred_element_type=jnp.float32,
            )
        degree = jnp.sum(count.astype(jnp.float32), axis=1, keepdims=True)
        agg = (acc * lax.rsqrt(1.0 + degree)).astype(jnp.bfloat16)
        rows = pl.ds(pl.multiple_of(b * BLOCK, BLOCK), BLOCK)
        agg_ref[rows, :] = agg
        qkv_ref[:, rows] = lax.dot_general(
            wt_ref[...], agg, (((1,), (1,)), ((), ())), preferred_element_type=jnp.float32
        ).astype(jnp.bfloat16)
        return carry

    lax.fori_loop(0, blocks, one_block, 0)


def aggregate(slots, serve, pattern, own, weight_t, pieces):
    rows, width = own.shape
    blocks = pattern.shape[0]
    return pl.pallas_call(
        aggregate_kernel,
        out_shape=(
            jax.ShapeDtypeStruct((rows, width), jnp.bfloat16),
            jax.ShapeDtypeStruct((weight_t.shape[0], rows), jnp.bfloat16),
        ),
        in_specs=[SM, SM, VM, VM, VM] + [ANY] * len(pieces),
        out_specs=(VM, VM),
        scratch_shapes=[
            pltpu.VMEM((blocks + len(pieces) - 2, BLOCK, width), jnp.bfloat16),
            pltpu.SemaphoreType.DMA((len(pieces) - 2,)),
        ],
        name="aggregate",
    )(slots, serve, pattern, own, weight_t, *pieces)


def attend_kernel(key_ref, qkv_ref, out_ref, q_ref, kv_ref):
    sources, _, rows = qkv_ref.shape
    per = rows // BLOCK
    keys = key_ref.shape[1]

    def unpack(h, carry):
        for j in range(per):
            cols = slice(j * BLOCK, (j + 1) * BLOCK)
            q_ref[h * per + j] = qkv_ref[h, 0:HDIM, cols]
            kv_ref[h * per + j] = qkv_ref[h, HDIM : 3 * HDIM, cols]
        return carry

    lax.fori_loop(0, sources, unpack, 0)
    ones = jnp.ones((16, keys * BLOCK), jnp.bfloat16)

    def one_block(b):
        ids = [key_ref[b, k] for k in range(keys)]
        key_t = jnp.concatenate([kv_ref[i, 0:HDIM, :] for i in ids], axis=1)
        value_t = jnp.concatenate([kv_ref[i, HDIM : 2 * HDIM, :] for i in ids], axis=1)
        scores = lax.dot_general(
            q_ref[b], key_t, (((0,), (0,)), ((), ())), preferred_element_type=jnp.float32
        )
        top = jnp.max(scores, axis=1, keepdims=True)
        terms = jnp.exp2((scores - top) * EXP2_SCALE).astype(jnp.bfloat16)
        mixed = lax.dot_general(
            jnp.concatenate([value_t, ones], axis=0),
            terms,
            (((1,), (1,)), ((), ())),
            preferred_element_type=jnp.float32,
        )
        return (mixed[0:HDIM] * (1.0 / mixed[HDIM : HDIM + 1])).astype(jnp.bfloat16)

    def one_source(h, carry):
        for j in range(per):
            out_ref[h, :, j * BLOCK : (j + 1) * BLOCK] = one_block(h * per + j)
        return carry

    lax.fori_loop(0, sources, one_source, 0)


def attend(key_blocks, qkv):
    sources, _, rows = qkv.shape
    blocks = sources * (rows // BLOCK)
    return pl.pallas_call(
        attend_kernel,
        out_shape=jax.ShapeDtypeStruct((sources, HDIM, rows), jnp.bfloat16),
        in_specs=[SM, VM],
        out_specs=VM,
        scratch_shapes=[
            pltpu.VMEM((blocks, HDIM, BLOCK), jnp.bfloat16),
            pltpu.VMEM((blocks, 2 * HDIM, BLOCK), jnp.bfloat16),
        ],
        name="attend",
    )(key_blocks, qkv)


def finish_kernel(context_ref, agg_ref, attn_ref, gain_ref, ffn_ref, out_ref, work_ref):
    rows, width = agg_ref.shape
    work_ref[...] = context_ref[...].T

    def one_block(b, carry):
        span = pl.ds(pl.multiple_of(b * BLOCK, BLOCK), BLOCK)
        mixed = agg_ref[span, :].astype(jnp.float32) + jnp.dot(
            work_ref[span, :], attn_ref[...], preferred_element_type=jnp.float32
        )
        mean_square = jnp.mean(mixed * mixed, axis=1, keepdims=True)
        normed = (mixed * lax.rsqrt(mean_square + 1e-06) * gain_ref[...]).astype(jnp.bfloat16)
        hidden = lax.dot_general(
            normed, ffn_ref[:, 0:width], (((1,), (1,)), ((), ())),
            preferred_element_type=jnp.float32,
        )
        hidden = jax.nn.gelu(hidden).astype(jnp.bfloat16)
        total = normed.astype(jnp.float32) + jnp.dot(
            hidden, ffn_ref[:, width : 2 * width], preferred_element_type=jnp.float32
        )
        out_ref[span, :] = total.astype(jnp.bfloat16)
        return carry

    lax.fori_loop(0, rows // BLOCK, one_block, 0)


def finish(context_t, agg, attn_weight, gain, ffn):
    rows, width = agg.shape
    return pl.pallas_call(
        finish_kernel,
        out_shape=jax.ShapeDtypeStruct((rows, width), jnp.bfloat16),
        in_specs=[VM] * 5,
        out_specs=VM,
        scratch_shapes=[pltpu.VMEM((rows, width), jnp.bfloat16)],
        name="finish",
    )(context_t, agg, attn_weight, gain, ffn)


def shards(
    features,
    tile_pattern,
    tile_source,
    serve_list,
    key_blocks,
    qkv_weight,
    attn_weight,
    norm_gain,
    expand_weight,
    reduce_weight,
):
    blocks = tile_pattern.shape[0]
    n_dom, n_head = lax.axis_size("dom"), lax.axis_size("head")
    width = features.shape[1]
    rows = features.shape[0]

    served = lax.all_to_all(
        serve_list.reshape(n_dom, 1), "dom", split_axis=0, concat_axis=0, tiled=True
    ).reshape(n_dom)
    ffn = jnp.concatenate([expand_weight, reduce_weight], axis=1)
    ffn = lax.all_to_all(
        jnp.broadcast_to(ffn[None], (n_head,) + ffn.shape),
        "head", split_axis=0, concat_axis=0, tiled=True,
    ).reshape(-1, 2 * width)
    weight_t = qkv_weight.T
    serve = jnp.take(served, piece_sources(n_dom))
    entry = tile_source.reshape(-1)
    slots = jnp.where(
        entry < blocks, entry, blocks + piece_of_source(jnp.maximum(entry - blocks, 0), n_dom)
    )
    pieces, tied = ring_pieces(features, {4: (serve, slots, weight_t), 8: ffn})
    (serve, slots, weight_t), ffn = tied[4], tied[8]
    agg, qkv_t = aggregate(slots, serve, tile_pattern, features, weight_t, pieces)
    qkv = lax.all_to_all(
        qkv_t.reshape(n_head, 3 * HDIM, rows), "head", split_axis=0, concat_axis=0, tiled=True
    )
    context = attend(key_blocks, qkv)
    context_t = lax.all_to_all(
        context, "head", split_axis=0, concat_axis=0, tiled=True
    ).reshape(HEADS * HDIM, rows)
    return finish(context_t, agg, attn_weight, norm_gain.reshape(1, width), ffn)


def solution(mesh):
    placed = (
        P(("dom", "head"), None),
        P(("dom", "head"), None, None, None),
        P(("dom", "head"), None),
        P("dom", "head", None, None),
        P("dom", None),
        P(),
        P(),
        P(),
        P("head", None),
        P("head", None),
    )
    return jax.shard_map(
        shards, mesh=mesh, in_specs=placed, out_specs=P(("dom", "head"), None), check_vma=False
    )
```

```python
import math

import jax
import jax.numpy as jnp
from jax import lax
from jax.experimental import pallas as pl
from jax.experimental.pallas import tpu as pltpu
from jax.sharding import PartitionSpec as P


HEADS = 16
HDIM = 32
BLOCK = 128
VM = pl.BlockSpec(memory_space=pltpu.VMEM)
SM = pl.BlockSpec(memory_space=pltpu.SMEM)
FAR = pl.BlockSpec(memory_space=pltpu.HBM)
EXP2_SCALE = math.log2(math.e) / math.sqrt(HDIM)


def ring_pieces(x, jobs):
    results = [None] * len(jobs)
    n = lax.axis_size("dom")
    half = n // 4
    cut = x.shape[0] // 2

    def send(v, by):
        return lax.ppermute(v, "dom", [(i, (i + by) % n) for i in range(n)])

    def trade(v):
        return lax.ppermute(v, "dom", [(i, i ^ 1) for i in range(n)])

    up, down = [x], [x]
    up_t, down_t = [trade(x)], []
    for k in range(1, half + 1):
        u_in, d_in = lax.optimization_barrier((up[-1], down[-1]))
        for i, (_, last, _, _) in enumerate(jobs):
            if k == last:
                u_in, results[i] = lax.optimization_barrier((u_in, results[i]))
        if k == half:
            u_in, d_in = u_in[:cut], d_in[cut:]
        if k >= 3:
            u_in, up_t[k - 2] = lax.optimization_barrier((u_in, up_t[k - 2]))
            d_in, down_t[k - 3] = lax.optimization_barrier((d_in, down_t[k - 3]))
        up.append(send(u_in, 2))
        down.append(send(d_in, -2))
        up_t.append(trade(up[-1]))
        down_t.append(trade(down[-1]))
        for i, (first, _, work, operand) in enumerate(jobs):
            if k == first:
                up_t[-1], down_t[-1], operand = lax.optimization_barrier(
                    (up_t[-1], down_t[-1], operand)
                )
                results[i] = work(operand)
    whole = up[:half] + down[1:half] + up_t[:half] + down_t[: half - 1]
    return whole + [up[half], down[half], up_t[half], down_t[half - 1]], results


def piece_sources(d, n):
    core, z = d % 2, d // 2
    chips, half = n // 2, n // 4
    up = [2 * ((z + chips - k) % chips) + core for k in range(half + 1)]
    down = [2 * ((z + k) % chips) + core for k in range(half + 1)]
    near = up[:half] + down[1:half]
    flip = 1 - 2 * core
    return near + [p + flip for p in near] + [up[half], up[half] + flip]


def slot_of_entry(e, d, blocks, n):
    p = jnp.maximum(e - blocks, 0)
    core, z = d % 2, d // 2
    chips, half = n // 2, n // 4
    k = (z + chips - p // 2) % chips
    other = jnp.where((p % 2) == core, 0, 1)
    near = jnp.where(k < half, k, half - 1 + chips - k)
    piece = jnp.where(k == half, 2 * (2 * half - 1) + other, near + other * (2 * half - 1))
    return jnp.where(e < blocks, e, blocks + piece)


def aggregate_kernel(place_ref, entry_ref, serve_ref, pattern_ref, own_ref, wt_ref, *rest):
    pieces, (agg_ref, qkv_ref, table, sems) = rest[:-4], rest[-4:]
    blocks, tiles = pattern_ref.shape[0], pattern_ref.shape[1]
    whole, halves = pieces[:-4], pieces[-4:]
    n_dom = len(pieces) - 2
    d = place_ref[0]
    sources = piece_sources(d, n_dom)
    copies = []

    def copy_of(i, piece, block):
        start = pl.multiple_of(block * BLOCK, BLOCK)
        return pltpu.make_async_copy(
            piece.at[pl.ds(start, BLOCK), :], table.at[blocks + i], sems.at[i]
        )

    for i, piece in enumerate(whole):
        copies.append(copy_of(i, piece, serve_ref[sources[i]]))
        copies[-1].start()
    for i in range(2):
        slot, first = len(whole) + i, blocks // 2
        block = serve_ref[sources[slot]]

        @pl.when(block < first)
        def _(slot=slot, piece=halves[2 * i], block=block):
            copy_of(slot, piece, block).start()

        @pl.when(block >= first)
        def _(slot=slot, piece=halves[2 * i + 1], block=block - first):
            copy_of(slot, piece, block).start()

        copies.append(copy_of(slot, halves[2 * i], 0))
    for b in range(blocks):
        table[b] = own_ref[b * BLOCK : (b + 1) * BLOCK, :]
    for copy in copies:
        copy.wait()

    def one_block(b, carry):
        acc = table[b].astype(jnp.float32)
        count = jnp.zeros((BLOCK, BLOCK), jnp.int32)
        for t in range(0, tiles, 2):
            two = []
            for u in (t, t + 1):
                pattern = pattern_ref[b, u]
                count = count + pattern
                two.append(pattern.astype(jnp.float32).astype(jnp.bfloat16))
            rows = [
                table[slot_of_entry(entry_ref[b, u], d, blocks, n_dom)] for u in (t, t + 1)
            ]
            acc = acc + jnp.dot(
                jnp.concatenate(two, axis=1),
                jnp.concatenate(rows, axis=0),
                preferred_element_type=jnp.float32,
            )
        degree = jnp.sum(count.astype(jnp.float32), axis=1, keepdims=True)
        span = pl.ds(pl.multiple_of(b * BLOCK, BLOCK), BLOCK)
        agg_ref[span, :] = (acc * lax.rsqrt(1.0 + degree)).astype(jnp.bfloat16)
        return carry

    lax.fori_loop(0, blocks, one_block, 0)
    third = qkv_ref.shape[0] // 3

    def one_third(i, carry):
        span = pl.ds(pl.multiple_of(i * third, third), third)
        qkv_ref[span, :] = lax.dot_general(
            wt_ref[span, :], agg_ref[...], (((1,), (1,)), ((), ())),
            preferred_element_type=jnp.float32,
        ).astype(jnp.bfloat16)
        return carry

    lax.fori_loop(0, 3, one_third, 0)


def aggregate(place, entries, serve, pattern, own, weight_t, pieces):
    rows, width = own.shape
    blocks, tiles = pattern.shape[0], pattern.shape[1]
    assert tiles % 2 == 0
    return pl.pallas_call(
        aggregate_kernel,
        out_shape=(
            jax.ShapeDtypeStruct((rows, width), jnp.bfloat16),
            jax.ShapeDtypeStruct((weight_t.shape[0], rows), jnp.bfloat16),
        ),
        in_specs=[SM, SM, SM, VM, VM, VM] + [FAR] * len(pieces),
        out_specs=(VM, VM),
        scratch_shapes=[
            pltpu.VMEM((blocks + len(pieces) - 2, BLOCK, width), jnp.bfloat16),
            pltpu.SemaphoreType.DMA((len(pieces) - 2,)),
        ],
        name="aggregate",
    )(place, entries, serve, pattern, own, weight_t, *pieces)


def attend_kernel(key_ref, qkv_ref, out_ref, q_ref, kv_ref):
    sources, _, rows = qkv_ref.shape
    per = rows // BLOCK
    keys = key_ref.shape[1]

    def unpack(h, carry):
        for j in range(per):
            cols = slice(j * BLOCK, (j + 1) * BLOCK)
            q_ref[h * per + j] = qkv_ref[h, 0:HDIM, cols]
            kv_ref[h * per + j] = qkv_ref[h, HDIM : 3 * HDIM, cols]
        return carry

    lax.fori_loop(0, sources, unpack, 0)
    ones = jnp.ones((16, keys * BLOCK), jnp.bfloat16)

    def chosen(b, part):
        span = slice(part * HDIM, (part + 1) * HDIM)
        return jnp.concatenate([kv_ref[key_ref[b, k], span, :] for k in range(keys)], axis=1)

    def probabilities(scores):
        top = jnp.max(scores, axis=1, keepdims=True)
        return jnp.exp2((scores - top) * EXP2_SCALE).astype(jnp.bfloat16)

    def one_source(h, carry):
        ids = [h * per + j for j in range(per)]
        scores = [
            lax.dot_general(
                q_ref[b], chosen(b, 0), (((0,), (0,)), ((), ())),
                preferred_element_type=jnp.float32,
            )
            for b in ids
        ]
        values = [jnp.concatenate([chosen(b, 1), ones], axis=0) for b in ids]
        terms = [probabilities(s) for s in scores]
        for j in range(per):
            mixed = lax.dot_general(
                values[j], terms[j], (((1,), (1,)), ((), ())),
                preferred_element_type=jnp.float32,
            )
            mixed = mixed[0:HDIM] * (1.0 / mixed[HDIM : HDIM + 1])
            out_ref[h, :, j * BLOCK : (j + 1) * BLOCK] = mixed.astype(jnp.bfloat16)
        return carry

    lax.fori_loop(0, sources, one_source, 0)


def attend(key_blocks, qkv):
    sources, _, rows = qkv.shape
    blocks = sources * (rows // BLOCK)
    return pl.pallas_call(
        attend_kernel,
        out_shape=jax.ShapeDtypeStruct((sources, HDIM, rows), jnp.bfloat16),
        in_specs=[SM, VM],
        out_specs=VM,
        scratch_shapes=[
            pltpu.VMEM((blocks, HDIM, BLOCK), jnp.bfloat16),
            pltpu.VMEM((blocks, 2 * HDIM, BLOCK), jnp.bfloat16),
        ],
        compiler_params=pltpu.CompilerParams(vmem_limit_bytes=16 << 20),
        name="attend",
    )(key_blocks, qkv)


def finish_kernel(context_ref, agg_ref, attn_ref, gain_ref, ffn_ref, out_ref, normed_ref, total_ref):
    _, width = agg_ref.shape
    hidden_units = ffn_ref.shape[0]
    mixed = agg_ref[...].astype(jnp.float32) + jnp.dot(
        context_ref[...].T, attn_ref[...], preferred_element_type=jnp.float32
    )
    mean_square = jnp.mean(mixed * mixed, axis=1, keepdims=True)
    normed = (mixed * lax.rsqrt(mean_square + 1e-06) * gain_ref[...]).astype(jnp.bfloat16)
    normed_ref[...] = normed
    total_ref[...] = normed.astype(jnp.float32)
    chunk = 512

    def one_chunk(c, carry):
        span = pl.ds(pl.multiple_of(c * chunk, chunk), chunk)
        hidden = lax.dot_general(
            normed_ref[...], ffn_ref[span, 0:width], (((1,), (1,)), ((), ())),
            preferred_element_type=jnp.float32,
        )
        hidden = jax.nn.gelu(hidden).astype(jnp.bfloat16)
        total_ref[...] += jnp.dot(
            hidden, ffn_ref[span, width : 2 * width], preferred_element_type=jnp.float32
        )
        return carry

    lax.fori_loop(0, hidden_units // chunk, one_chunk, 0)
    out_ref[...] = total_ref[...].astype(jnp.bfloat16)


def finish(context_t, agg, attn_weight, gain, ffn):
    rows, width = agg.shape
    return pl.pallas_call(
        finish_kernel,
        out_shape=jax.ShapeDtypeStruct((rows, width), jnp.bfloat16),
        in_specs=[VM] * 5,
        out_specs=VM,
        scratch_shapes=[
            pltpu.VMEM((rows, width), jnp.bfloat16),
            pltpu.VMEM((rows, width), jnp.float32),
        ],
        compiler_params=pltpu.CompilerParams(vmem_limit_bytes=20 << 20),
        name="finish",
    )(context_t, agg, attn_weight, gain, ffn)


def shards(
    features,
    tile_pattern,
    tile_source,
    serve_list,
    key_blocks,
    qkv_weight,
    attn_weight,
    norm_gain,
    expand_weight,
    reduce_weight,
):
    n_dom, n_head = lax.axis_size("dom"), lax.axis_size("head")
    width = features.shape[1]
    rows = features.shape[0]

    def exchange_lists(lists):
        return lax.all_to_all(
            lists.reshape(n_dom, 1), "dom", split_axis=0, concat_axis=0, tiled=True
        ).reshape(n_dom)

    def gather_ffn(weights):
        both = jnp.concatenate(weights, axis=1)
        return lax.all_to_all(
            jnp.broadcast_to(both[None], (n_head,) + both.shape),
            "head", split_axis=0, concat_axis=0, tiled=True,
        ).reshape(-1, 2 * width)

    jobs = [
        (1, 5, exchange_lists, serve_list),
        (2, None, gather_ffn, (expand_weight, reduce_weight)),
        (4, 7, jnp.transpose, qkv_weight),
    ]
    pieces, (served, ffn, weight_t) = ring_pieces(features, jobs)
    place = lax.axis_index("dom").reshape(1)
    agg, qkv_t = aggregate(
        place, tile_source, served, tile_pattern, features, weight_t, pieces
    )
    qkv = lax.all_to_all(
        qkv_t.reshape(n_head, 3 * HDIM, rows), "head", split_axis=0, concat_axis=0, tiled=True
    )
    context = attend(key_blocks, qkv)
    context_t = lax.all_to_all(
        context, "head", split_axis=0, concat_axis=0, tiled=True
    ).reshape(HEADS * HDIM, rows)
    return finish(context_t, agg, attn_weight, norm_gain.reshape(1, width), ffn)


def solution(mesh):
    placed = (
        P(("dom", "head"), None),
        P(("dom", "head"), None, None, None),
        P(("dom", "head"), None),
        P("dom", "head", None, None),
        P("dom", None),
        P(),
        P(),
        P(),
        P("head", None),
        P("head", None),
    )

    return jax.shard_map(
        shards, mesh=mesh, in_specs=placed, out_specs=P(("dom", "head"), None), check_vma=False
    )
```

```python
import functools
import math

import jax
import jax.numpy as jnp
from jax import lax
from jax.experimental import pallas as pl
from jax.experimental.pallas import tpu as pltpu
from jax.sharding import PartitionSpec as P


HEADS = 16
HDIM = 32
BLOCK = 128
VM = pl.BlockSpec(memory_space=pltpu.VMEM)
SM = pl.BlockSpec(memory_space=pltpu.SMEM)
FAR = pl.BlockSpec(memory_space=pltpu.HBM)
EXP2_SCALE = math.log2(math.e) / math.sqrt(HDIM)


def pick_kernel(steps, place_ref, wanted_ref, *refs):
    pieces, out_ref, sems = refs[:-2], refs[-2], refs[-1]
    n = wanted_ref.shape[0]
    core, z = place_ref[0] % 2, place_ref[0] // 2
    chips = n // 2

    def copy_of(i, piece, block):
        rows = pl.ds(pl.multiple_of(block * BLOCK, BLOCK), BLOCK)
        return pltpu.make_async_copy(
            piece.at[rows, :], out_ref.at[pl.ds(i * BLOCK, BLOCK), :], sems.at[i]
        )

    def wanted(step):
        return wanted_ref[2 * ((z + chips - step) % chips) + core]

    if len(steps) < len(pieces):
        block, first = wanted(steps[0]), pieces[0].shape[0] // BLOCK

        @pl.when(block < first)
        def _():
            copy_of(0, pieces[0], block).start()

        @pl.when(block >= first)
        def _():
            copy_of(0, pieces[1], block - first).start()

        copy_of(0, pieces[0], 0).wait()
        return
    copies = [copy_of(i, pieces[i], wanted(step)) for i, step in enumerate(steps)]
    for copy in copies:
        copy.start()
    for copy in copies:
        copy.wait()


def pick(place, wanted, pieces, steps):
    width = pieces[0].shape[1]
    return pl.pallas_call(
        functools.partial(pick_kernel, steps),
        out_shape=jax.ShapeDtypeStruct((len(steps) * BLOCK, width), jnp.bfloat16),
        in_specs=[SM, SM] + [pl.BlockSpec(memory_space=pl.ANY)] * len(pieces),
        out_specs=VM,
        scratch_shapes=[pltpu.SemaphoreType.DMA((len(steps),))],
        compiler_params=pltpu.CompilerParams(vmem_limit_bytes=2 << 20),
        name="pick",
    )(place, wanted, *pieces)


def ring_pieces(x, place, lists, weights):
    n, n_head = lax.axis_size("dom"), lax.axis_size("head")
    half = n // 4
    cut = x.shape[0] // 2

    def send(v, by):
        return lax.ppermute(v, "dom", [(i, (i + by) % n) for i in range(n)])

    def trade(v):
        return lax.ppermute(v, "dom", [(i, i ^ 1) for i in range(n)])

    up, down, traded = [x], [x], []
    served = ffn = None
    for k in range(1, half + 1):
        u_in, d_in = lax.optimization_barrier((up[-1], down[-1]))
        if k == half:
            u_in, d_in = u_in[:cut], d_in[cut:]
        if k >= 4:
            u_in, d_in, traded[k - 3] = lax.optimization_barrier((u_in, d_in, traded[k - 3]))
        up.append(send(u_in, 2))
        down.append(send(d_in, -2))
        if k == 1:
            mine = lists.reshape(n)
            swapped = mine.reshape(n // 2, 2)[:, ::-1].reshape(n)
            served = lax.all_to_all(
                jnp.stack([mine, swapped], axis=1),
                "dom", split_axis=0, concat_axis=0, tiled=True,
            )
            served, wanted = served[:, 0], served[:, 1]
        if k == 2:
            traded.append(trade(pick(place, wanted, [x], [0])))
        if k == 3:
            both = jnp.concatenate(weights, axis=1)
            both, traded[0] = lax.optimization_barrier((both, traded[0]))
            ffn = lax.all_to_all(
                jnp.broadcast_to(both[None], (n_head,) + both.shape),
                "head", split_axis=0, concat_axis=0, tiled=True,
            )
        if k == half:
            last = pick(place, wanted, [up[-1], down[-1]], [half])
            traded.append(trade(last))
        elif k >= 2:
            if k == 2:
                traded.append(trade(pick(place, wanted, [up[1], down[1]], [1, n // 2 - 1])))
            pair = pick(place, wanted, [up[k], down[k]], [k, n // 2 - k])
            if k == half - 1:
                pair, ffn = lax.optimization_barrier((pair, ffn))
            traded.append(trade(pair))
    ffn = ffn.reshape(-1, ffn.shape[-1])
    return up[:half] + down[1:half], [up[half], down[half]], traded, served, ffn


def slot_of_entry(e, d, blocks, n):
    p = jnp.maximum(e - blocks, 0)
    core, z = d % 2, d // 2
    chips, half = n // 2, n // 4
    k = (z + chips - p // 2) % chips
    other = jnp.where((p % 2) == core, 0, chips)
    near = jnp.where(k < half, k, half - 1 + chips - k)
    near = jnp.where(k == half, chips - 1, near)
    return jnp.where(e < blocks, e, blocks + other + near)


def aggregate_kernel(place_ref, entry_ref, serve_ref, pattern_ref, own_ref, wt_ref, *rest):
    pieces, (agg_ref, qkv_ref, table, sems) = rest[:-4], rest[-4:]
    blocks, tiles = pattern_ref.shape[0], pattern_ref.shape[1]
    n_dom = serve_ref.shape[0]
    chips, half = n_dom // 2, n_dom // 4
    whole, halves, traded = pieces[: chips - 1], pieces[chips - 1 : chips + 1], pieces[chips + 1 :]
    d = place_ref[0]
    core, z = d % 2, d // 2
    copies = []

    def copy_of(slot, piece, block):
        rows = pl.ds(pl.multiple_of(block * BLOCK, BLOCK), BLOCK)
        return pltpu.make_async_copy(
            piece.at[rows, :], table.at[blocks + slot], sems.at[slot]
        )

    def served(step):
        return serve_ref[2 * ((z + chips - step) % chips) + core]

    steps = list(range(half)) + [chips - k for k in range(1, half)]
    for slot, (piece, step) in enumerate(zip(whole, steps)):
        copies.append(copy_of(slot, piece, served(step)))
        copies[-1].start()
    slot, first = chips - 1, blocks // 2
    block = served(half)

    @pl.when(block < first)
    def _():
        copy_of(slot, halves[0], block).start()

    @pl.when(block >= first)
    def _():
        copy_of(slot, halves[1], block - first).start()

    copies.append(copy_of(slot, halves[0], 0))
    handed = [(chips, traded[0], 0)]
    for k in range(1, half):
        handed += [(chips + k, traded[k], 0), (chips + half - 1 + k, traded[k], 1)]
    for slot, piece, block in handed + [(n_dom - 1, traded[half], 0)]:
        copies.append(copy_of(slot, piece, block))
        copies[-1].start()
    for b in range(blocks):
        table[b] = own_ref[b * BLOCK : (b + 1) * BLOCK, :]
    for copy in copies:
        copy.wait()

    def one_block(b, carry):
        acc = table[b].astype(jnp.float32)
        count = jnp.zeros((BLOCK, BLOCK), jnp.int32)
        for t in range(0, tiles, 2):
            two = []
            for u in (t, t + 1):
                pattern = pattern_ref[b, u]
                count = count + pattern
                two.append(pattern.astype(jnp.float32).astype(jnp.bfloat16))
            rows = [
                table[slot_of_entry(entry_ref[b, u], d, blocks, n_dom)] for u in (t, t + 1)
            ]
            acc = acc + jnp.dot(
                jnp.concatenate(two, axis=1),
                jnp.concatenate(rows, axis=0),
                preferred_element_type=jnp.float32,
            )
        degree = jnp.sum(count.astype(jnp.float32), axis=1, keepdims=True)
        span = pl.ds(pl.multiple_of(b * BLOCK, BLOCK), BLOCK)
        agg_ref[span, :] = (acc * lax.rsqrt(1.0 + degree)).astype(jnp.bfloat16)
        return carry

    lax.fori_loop(0, blocks, one_block, 0)
    third = qkv_ref.shape[0] // 3

    def one_third(i, carry):
        span = pl.ds(pl.multiple_of(i * third, third), third)
        qkv_ref[span, :] = lax.dot_general(
            wt_ref[span, :], agg_ref[...], (((1,), (1,)), ((), ())),
            preferred_element_type=jnp.float32,
        ).astype(jnp.bfloat16)
        return carry

    lax.fori_loop(0, 3, one_third, 0)


def aggregate(place, entries, serve, pattern, own, weight_t, pieces):
    rows, width = own.shape
    blocks, tiles = pattern.shape[0], pattern.shape[1]
    assert tiles % 2 == 0
    return pl.pallas_call(
        aggregate_kernel,
        out_shape=(
            jax.ShapeDtypeStruct((rows, width), jnp.bfloat16),
            jax.ShapeDtypeStruct((weight_t.shape[0], rows), jnp.bfloat16),
        ),
        in_specs=[SM, SM, SM, VM, VM, VM] + [FAR] * len(pieces),
        out_specs=(VM, VM),
        scratch_shapes=[
            pltpu.VMEM((blocks + serve.shape[0], BLOCK, width), jnp.bfloat16),
            pltpu.SemaphoreType.DMA((serve.shape[0],)),
        ],
        name="aggregate",
    )(place, entries, serve, pattern, own, weight_t, *pieces)


def attend_kernel(key_ref, qkv_ref, out_ref, q_ref, kv_ref):
    sources, _, rows = qkv_ref.shape
    per = rows // BLOCK
    keys = key_ref.shape[1]

    def unpack(h, carry):
        for j in range(per):
            cols = slice(j * BLOCK, (j + 1) * BLOCK)
            q_ref[h * per + j] = qkv_ref[h, 0:HDIM, cols]
            kv_ref[h * per + j] = qkv_ref[h, HDIM : 3 * HDIM, cols]
        return carry

    lax.fori_loop(0, sources, unpack, 0)
    ones = jnp.ones((16, keys * BLOCK), jnp.bfloat16)

    def chosen(b, part):
        span = slice(part * HDIM, (part + 1) * HDIM)
        return jnp.concatenate([kv_ref[key_ref[b, k], span, :] for k in range(keys)], axis=1)

    def probabilities(scores):
        top = jnp.max(scores, axis=1, keepdims=True)
        return jnp.exp2((scores - top) * EXP2_SCALE).astype(jnp.bfloat16)

    def one_source(h, carry):
        ids = [h * per + j for j in range(per)]
        scores = [
            lax.dot_general(
                q_ref[b], chosen(b, 0), (((0,), (0,)), ((), ())),
                preferred_element_type=jnp.float32,
            )
            for b in ids
        ]
        values = [jnp.concatenate([chosen(b, 1), ones], axis=0) for b in ids]
        terms = [probabilities(s) for s in scores]
        for j in range(per):
            mixed = lax.dot_general(
                values[j], terms[j], (((1,), (1,)), ((), ())),
                preferred_element_type=jnp.float32,
            )
            mixed = mixed[0:HDIM] * (1.0 / mixed[HDIM : HDIM + 1])
            out_ref[h, :, j * BLOCK : (j + 1) * BLOCK] = mixed.astype(jnp.bfloat16)
        return carry

    lax.fori_loop(0, sources, one_source, 0)


def attend(key_blocks, qkv):
    sources, _, rows = qkv.shape
    blocks = sources * (rows // BLOCK)
    return pl.pallas_call(
        attend_kernel,
        out_shape=jax.ShapeDtypeStruct((sources, HDIM, rows), jnp.bfloat16),
        in_specs=[SM, VM],
        out_specs=VM,
        scratch_shapes=[
            pltpu.VMEM((blocks, HDIM, BLOCK), jnp.bfloat16),
            pltpu.VMEM((blocks, 2 * HDIM, BLOCK), jnp.bfloat16),
        ],
        compiler_params=pltpu.CompilerParams(vmem_limit_bytes=16 << 20),
        name="attend",
    )(key_blocks, qkv)


def finish_kernel(context_ref, agg_ref, attn_ref, gain_ref, ffn_ref, out_ref, normed_ref, total_ref):
    _, width = agg_ref.shape
    hidden_units = ffn_ref.shape[0]
    mixed = agg_ref[...].astype(jnp.float32) + jnp.dot(
        context_ref[...].T, attn_ref[...], preferred_element_type=jnp.float32
    )
    mean_square = jnp.mean(mixed * mixed, axis=1, keepdims=True)
    normed = (mixed * lax.rsqrt(mean_square + 1e-06) * gain_ref[...]).astype(jnp.bfloat16)
    normed_ref[...] = normed
    total_ref[...] = normed.astype(jnp.float32)
    chunk = 512

    def one_chunk(c, carry):
        span = pl.ds(pl.multiple_of(c * chunk, chunk), chunk)
        hidden = lax.dot_general(
            normed_ref[...], ffn_ref[span, 0:width], (((1,), (1,)), ((), ())),
            preferred_element_type=jnp.float32,
        )
        hidden = jax.nn.gelu(hidden).astype(jnp.bfloat16)
        total_ref[...] += jnp.dot(
            hidden, ffn_ref[span, width : 2 * width], preferred_element_type=jnp.float32
        )
        return carry

    lax.fori_loop(0, hidden_units // chunk, one_chunk, 0)
    out_ref[...] = total_ref[...].astype(jnp.bfloat16)


def finish(context_t, agg, attn_weight, gain, ffn):
    rows, width = agg.shape
    return pl.pallas_call(
        finish_kernel,
        out_shape=jax.ShapeDtypeStruct((rows, width), jnp.bfloat16),
        in_specs=[VM] * 5,
        out_specs=VM,
        scratch_shapes=[
            pltpu.VMEM((rows, width), jnp.bfloat16),
            pltpu.VMEM((rows, width), jnp.float32),
        ],
        compiler_params=pltpu.CompilerParams(vmem_limit_bytes=20 << 20),
        name="finish",
    )(context_t, agg, attn_weight, gain, ffn)


def shards(
    features,
    tile_pattern,
    tile_source,
    serve_list,
    key_blocks,
    qkv_weight,
    attn_weight,
    norm_gain,
    expand_weight,
    reduce_weight,
):
    n_head = lax.axis_size("head")
    width = features.shape[1]
    rows = features.shape[0]

    place = lax.axis_index("dom").reshape(1)
    whole, halves, traded, served, ffn = ring_pieces(
        features, place, serve_list, (expand_weight, reduce_weight)
    )
    weight_t = qkv_weight.T
    agg, qkv_t = aggregate(
        place, tile_source, served, tile_pattern, features, weight_t, whole + halves + traded
    )
    qkv = lax.all_to_all(
        qkv_t.reshape(n_head, 3 * HDIM, rows), "head", split_axis=0, concat_axis=0, tiled=True
    )
    context = attend(key_blocks, qkv)
    context_t = lax.all_to_all(
        context, "head", split_axis=0, concat_axis=0, tiled=True
    ).reshape(HEADS * HDIM, rows)
    return finish(context_t, agg, attn_weight, norm_gain.reshape(1, width), ffn)


def solution(mesh):
    placed = (
        P(("dom", "head"), None),
        P(("dom", "head"), None, None, None),
        P(("dom", "head"), None),
        P("dom", "head", None, None),
        P("dom", None),
        P(),
        P(),
        P(),
        P("head", None),
        P("head", None),
    )

    return jax.shard_map(
        shards, mesh=mesh, in_specs=placed, out_specs=P(("dom", "head"), None), check_vma=False
    )
```

```python
import math

import jax
import jax.numpy as jnp
from jax import lax
from jax.experimental import pallas as pl
from jax.experimental.pallas import tpu as pltpu
from jax.sharding import PartitionSpec as P


HEADS = 16
HDIM = 32
BLOCK = 128
VM = pl.BlockSpec(memory_space=pltpu.VMEM)
SM = pl.BlockSpec(memory_space=pltpu.SMEM)
FAR = pl.BlockSpec(memory_space=pltpu.HBM)
EXP2_SCALE = math.log2(math.e) / math.sqrt(HDIM)


def start_copies(place_ref, wanted_ref, whole, halves, slot_of, sems):
    n = wanted_ref.shape[0]
    core, z = place_ref[0] % 2, place_ref[0] // 2
    chips, half = n // 2, n // 4
    copies = []

    def copy_of(slot, piece, block):
        rows = pl.ds(pl.multiple_of(block * BLOCK, BLOCK), BLOCK)
        return pltpu.make_async_copy(piece.at[rows, :], slot_of(slot), sems.at[slot])

    def wanted(step):
        return wanted_ref[2 * ((z + chips - step) % chips) + core]

    steps = list(range(half)) + [chips - k for k in range(1, half)]
    for slot, (piece, step) in enumerate(zip(whole, steps)):
        copies.append(copy_of(slot, piece, wanted(step)))
        copies[-1].start()
    slot, first = chips - 1, halves[0].shape[0] // BLOCK
    block = wanted(half)

    @pl.when(block < first)
    def _():
        copy_of(slot, halves[0], block).start()

    @pl.when(block >= first)
    def _():
        copy_of(slot, halves[1], block - first).start()

    copies.append(copy_of(slot, halves[0], 0))
    return copies


def pick_kernel(place_ref, wanted_ref, *refs):
    whole, halves, (out_ref, sems) = refs[:-4], refs[-4:-2], refs[-2:]
    for copy in start_copies(
        place_ref, wanted_ref, whole, halves, lambda slot: out_ref.at[slot], sems
    ):
        copy.wait()


def pick(place, wanted, whole, halves):
    slots = len(whole) + 1
    return pl.pallas_call(
        pick_kernel,
        out_shape=jax.ShapeDtypeStruct((slots, BLOCK, whole[0].shape[1]), jnp.bfloat16),
        in_specs=[SM, SM] + [FAR] * (len(whole) + 2),
        out_specs=VM,
        scratch_shapes=[pltpu.SemaphoreType.DMA((slots,))],
        name="pick",
    )(place, wanted, *whole, *halves)


def ring_pieces(x, lists, weights, qkv_weight):
    n, n_head = lax.axis_size("dom"), lax.axis_size("head")
    half = n // 4
    cut = x.shape[0] // 2

    def send(v, by):
        return lax.ppermute(v, "dom", [(i, (i + by) % n) for i in range(n)])

    up, down = [x], [x]
    weight_t = qkv_weight.T
    mine = lists.reshape(n)
    swapped = mine.reshape(n // 2, 2)[:, ::-1].reshape(n)
    served = lax.all_to_all(
        jnp.stack([mine, swapped], axis=1), "dom", split_axis=0, concat_axis=0, tiled=True
    )
    both = jnp.concatenate(weights, axis=1)
    both, served = lax.optimization_barrier((both, served))
    ffn = lax.all_to_all(
        jnp.broadcast_to(both[None], (n_head,) + both.shape),
        "head", split_axis=0, concat_axis=0, tiled=True,
    ).reshape(-1, both.shape[1])
    for k in range(1, half + 1):
        u_in, d_in = up[-1], down[-1]
        if k == half:
            u_in, d_in = u_in[:cut], d_in[cut:]
        if k == 6:
            u_in, weight_t = lax.optimization_barrier((u_in, weight_t))
        if k == half:
            u_in, ffn = lax.optimization_barrier((u_in, ffn))
        up.append(send(u_in, 2))
        down.append(send(d_in, -2))
    return up[:half] + down[1:half], [up[half], down[half]], served, ffn, weight_t


def slot_of_entry(e, d, blocks, n):
    p = jnp.maximum(e - blocks, 0)
    core, z = d % 2, d // 2
    chips, half = n // 2, n // 4
    k = (z + chips - p // 2) % chips
    other = jnp.where((p % 2) == core, 0, chips)
    near = jnp.where(k < half, k, half - 1 + chips - k)
    near = jnp.where(k == half, chips - 1, near)
    return jnp.where(e < blocks, e, blocks + other + near)


def aggregate_kernel(place_ref, entry_ref, serve_ref, pattern_ref, own_ref, wt_ref, *rest):
    pieces, (agg_ref, qkv_ref, table, sems) = rest[:-4], rest[-4:]
    blocks, tiles = pattern_ref.shape[0], pattern_ref.shape[1]
    n_dom = serve_ref.shape[0]
    chips = n_dom // 2
    d = place_ref[0]
    copies = start_copies(
        place_ref, serve_ref, pieces[:-3], pieces[-3:-1], lambda slot: table.at[blocks + slot], sems
    )
    handed = pltpu.make_async_copy(
        pieces[-1], table.at[pl.ds(blocks + chips, chips)], sems.at[chips]
    )
    handed.start()
    copies.append(handed)
    for b in range(blocks):
        table[b] = own_ref[b * BLOCK : (b + 1) * BLOCK, :]
    for copy in copies:
        copy.wait()

    def one_block(b, carry):
        acc = table[b].astype(jnp.float32)
        count = jnp.zeros((BLOCK, BLOCK), jnp.int32)
        for t in range(0, tiles, 2):
            two = []
            for u in (t, t + 1):
                pattern = pattern_ref[b, u]
                count = count + pattern
                two.append(pattern.astype(jnp.float32).astype(jnp.bfloat16))
            rows = [
                table[slot_of_entry(entry_ref[b, u], d, blocks, n_dom)] for u in (t, t + 1)
            ]
            acc = acc + jnp.dot(
                jnp.concatenate(two, axis=1),
                jnp.concatenate(rows, axis=0),
                preferred_element_type=jnp.float32,
            )
        degree = jnp.sum(count.astype(jnp.float32), axis=1, keepdims=True)
        span = pl.ds(pl.multiple_of(b * BLOCK, BLOCK), BLOCK)
        agg_ref[span, :] = (acc * lax.rsqrt(1.0 + degree)).astype(jnp.bfloat16)
        return carry

    lax.fori_loop(0, blocks, one_block, 0)
    third = qkv_ref.shape[0] // 3

    def one_third(i, carry):
        span = pl.ds(pl.multiple_of(i * third, third), third)
        qkv_ref[span, :] = lax.dot_general(
            wt_ref[span, :], agg_ref[...], (((1,), (1,)), ((), ())),
            preferred_element_type=jnp.float32,
        ).astype(jnp.bfloat16)
        return carry

    lax.fori_loop(0, 3, one_third, 0)


def aggregate(place, entries, serve, pattern, own, weight_t, pieces):
    rows, width = own.shape
    blocks, tiles = pattern.shape[0], pattern.shape[1]
    assert tiles % 2 == 0
    return pl.pallas_call(
        aggregate_kernel,
        out_shape=(
            jax.ShapeDtypeStruct((rows, width), jnp.bfloat16),
            jax.ShapeDtypeStruct((weight_t.shape[0], rows), jnp.bfloat16),
        ),
        in_specs=[SM, SM, SM, VM, VM, VM] + [FAR] * len(pieces),
        out_specs=(VM, VM),
        scratch_shapes=[
            pltpu.VMEM((blocks + serve.shape[0], BLOCK, width), jnp.bfloat16),
            pltpu.SemaphoreType.DMA((serve.shape[0] // 2 + 1,)),
        ],
        name="aggregate",
    )(place, entries, serve, pattern, own, weight_t, *pieces)


def attend_kernel(key_ref, qkv_ref, out_ref, q_ref, kv_ref):
    sources, _, rows = qkv_ref.shape
    per = rows // BLOCK
    keys = key_ref.shape[1]

    def unpack(h, carry):
        for j in range(per):
            cols = slice(j * BLOCK, (j + 1) * BLOCK)
            q_ref[h * per + j] = qkv_ref[h, 0:HDIM, cols]
            kv_ref[h * per + j] = qkv_ref[h, HDIM : 3 * HDIM, cols]
        return carry

    lax.fori_loop(0, sources, unpack, 0)
    ones = jnp.ones((16, keys * BLOCK), jnp.bfloat16)

    def chosen(b, part):
        span = slice(part * HDIM, (part + 1) * HDIM)
        return jnp.concatenate([kv_ref[key_ref[b, k], span, :] for k in range(keys)], axis=1)

    def probabilities(scores):
        top = jnp.max(scores, axis=1, keepdims=True)
        return jnp.exp2((scores - top) * EXP2_SCALE).astype(jnp.bfloat16)

    def one_source(h, carry):
        ids = [h * per + j for j in range(per)]
        scores = [
            lax.dot_general(
                q_ref[b], chosen(b, 0), (((0,), (0,)), ((), ())),
                preferred_element_type=jnp.float32,
            )
            for b in ids
        ]
        values = [jnp.concatenate([chosen(b, 1), ones], axis=0) for b in ids]
        terms = [probabilities(s) for s in scores]
        for j in range(per):
            mixed = lax.dot_general(
                values[j], terms[j], (((1,), (1,)), ((), ())),
                preferred_element_type=jnp.float32,
            )
            mixed = mixed[0:HDIM] * (1.0 / mixed[HDIM : HDIM + 1])
            out_ref[h, :, j * BLOCK : (j + 1) * BLOCK] = mixed.astype(jnp.bfloat16)
        return carry

    lax.fori_loop(0, sources, one_source, 0)


def attend(key_blocks, qkv):
    sources, _, rows = qkv.shape
    blocks = sources * (rows // BLOCK)
    return pl.pallas_call(
        attend_kernel,
        out_shape=jax.ShapeDtypeStruct((sources, HDIM, rows), jnp.bfloat16),
        in_specs=[SM, VM],
        out_specs=VM,
        scratch_shapes=[
            pltpu.VMEM((blocks, HDIM, BLOCK), jnp.bfloat16),
            pltpu.VMEM((blocks, 2 * HDIM, BLOCK), jnp.bfloat16),
        ],
        compiler_params=pltpu.CompilerParams(vmem_limit_bytes=16 << 20),
        name="attend",
    )(key_blocks, qkv)


def finish_kernel(context_ref, agg_ref, attn_ref, gain_ref, ffn_ref, out_ref, normed_ref, total_ref):
    _, width = agg_ref.shape
    hidden_units = ffn_ref.shape[0]
    mixed = agg_ref[...].astype(jnp.float32) + jnp.dot(
        context_ref[...].T, attn_ref[...], preferred_element_type=jnp.float32
    )
    mean_square = jnp.mean(mixed * mixed, axis=1, keepdims=True)
    normed = (mixed * lax.rsqrt(mean_square + 1e-06) * gain_ref[...]).astype(jnp.bfloat16)
    normed_ref[...] = normed
    total_ref[...] = normed.astype(jnp.float32)
    chunk = 512

    def one_chunk(c, carry):
        span = pl.ds(pl.multiple_of(c * chunk, chunk), chunk)
        hidden = lax.dot_general(
            normed_ref[...], ffn_ref[span, 0:width], (((1,), (1,)), ((), ())),
            preferred_element_type=jnp.float32,
        )
        hidden = jax.nn.gelu(hidden).astype(jnp.bfloat16)
        total_ref[...] += jnp.dot(
            hidden, ffn_ref[span, width : 2 * width], preferred_element_type=jnp.float32
        )
        return carry

    lax.fori_loop(0, hidden_units // chunk, one_chunk, 0)
    out_ref[...] = total_ref[...].astype(jnp.bfloat16)


def finish(context_t, agg, attn_weight, gain, ffn):
    rows, width = agg.shape
    return pl.pallas_call(
        finish_kernel,
        out_shape=jax.ShapeDtypeStruct((rows, width), jnp.bfloat16),
        in_specs=[VM] * 5,
        out_specs=VM,
        scratch_shapes=[
            pltpu.VMEM((rows, width), jnp.bfloat16),
            pltpu.VMEM((rows, width), jnp.float32),
        ],
        compiler_params=pltpu.CompilerParams(vmem_limit_bytes=20 << 20),
        name="finish",
    )(context_t, agg, attn_weight, gain, ffn)


def shards(
    features,
    tile_pattern,
    tile_source,
    serve_list,
    key_blocks,
    qkv_weight,
    attn_weight,
    norm_gain,
    expand_weight,
    reduce_weight,
):
    n_head = lax.axis_size("head")
    width = features.shape[1]
    rows = features.shape[0]

    place = lax.axis_index("dom").reshape(1)
    n_dom = lax.axis_size("dom")
    whole, halves, served, ffn, weight_t = ring_pieces(
        features, serve_list, (expand_weight, reduce_weight), qkv_weight
    )
    handed = lax.ppermute(
        pick(place, served[:, 1], whole, halves), "dom", [(i, i ^ 1) for i in range(n_dom)]
    )
    agg, qkv_t = aggregate(
        place, tile_source, served[:, 0], tile_pattern, features, weight_t,
        whole + halves + [handed],
    )
    qkv = lax.all_to_all(
        qkv_t.reshape(n_head, 3 * HDIM, rows), "head", split_axis=0, concat_axis=0, tiled=True
    )
    context = attend(key_blocks, qkv)
    context_t = lax.all_to_all(
        context, "head", split_axis=0, concat_axis=0, tiled=True
    ).reshape(HEADS * HDIM, rows)
    return finish(context_t, agg, attn_weight, norm_gain.reshape(1, width), ffn)


def solution(mesh):
    placed = (
        P(("dom", "head"), None),
        P(("dom", "head"), None, None, None),
        P(("dom", "head"), None),
        P("dom", "head", None, None),
        P("dom", None),
        P(),
        P(),
        P(),
        P("head", None),
        P("head", None),
    )

    return jax.shard_map(
        shards, mesh=mesh, in_specs=placed, out_specs=P(("dom", "head"), None), check_vma=False
    )
```

```python
import math

import jax
import jax.numpy as jnp
from jax import lax
from jax.experimental import pallas as pl
from jax.experimental.pallas import tpu as pltpu
from jax.sharding import PartitionSpec as P


HEADS = 16
HDIM = 32
BLOCK = 128
VM = pl.BlockSpec(memory_space=pltpu.VMEM)
SM = pl.BlockSpec(memory_space=pltpu.SMEM)
FAR = pl.BlockSpec(memory_space=pltpu.HBM)
EXP2_SCALE = math.log2(math.e) / math.sqrt(HDIM)


def start_copies(place_ref, wanted_ref, far_row, pieces, slot_of, sems):
    n = wanted_ref.shape[0]
    core, z = place_ref[0] % 2, place_ref[0] // 2
    chips, half = n // 2, n // 4
    copies = []
    steps = list(range(half)) + [chips - k for k in range(1, half)] + [half]
    for slot, (piece, step) in enumerate(zip(pieces, steps)):
        block = wanted_ref[2 * ((z + chips - step) % chips) + core]
        if step == half:
            block = far_row
        rows = pl.ds(pl.multiple_of(block * BLOCK, BLOCK), BLOCK)
        copies.append(pltpu.make_async_copy(piece.at[rows, :], slot_of(slot), sems.at[slot]))
        copies[-1].start()
    return copies


def pick_kernel(place_ref, wanted_ref, *refs):
    pieces, (out_ref, sems) = refs[:-2], refs[-2:]
    for copy in start_copies(
        place_ref, wanted_ref, 1, pieces, lambda slot: out_ref.at[slot], sems
    ):
        copy.wait()


def pick(place, wanted, pieces):
    return pl.pallas_call(
        pick_kernel,
        out_shape=jax.ShapeDtypeStruct((len(pieces), BLOCK, pieces[0].shape[1]), jnp.bfloat16),
        in_specs=[SM, SM] + [FAR] * len(pieces),
        out_specs=VM,
        scratch_shapes=[pltpu.SemaphoreType.DMA((len(pieces),))],
        name="pick",
    )(place, wanted, *pieces)


def pass_on_kernel(place_ref, mine_ref, other_ref, piece, out_ref, sems):
    n = mine_ref.shape[0]
    core, z = place_ref[0] % 2, place_ref[0] // 2
    chips, half = n // 2, n // 4
    source = 2 * ((z + chips - (half - 1)) % chips) + core
    copies = []
    for i, ref in enumerate((mine_ref, other_ref)):
        rows = pl.ds(pl.multiple_of(ref[source] * BLOCK, BLOCK), BLOCK)
        copies.append(
            pltpu.make_async_copy(
                piece.at[rows, :], out_ref.at[pl.ds(i * BLOCK, BLOCK), :], sems.at[i]
            )
        )
        copies[-1].start()
    for copy in copies:
        copy.wait()


def pass_on(place, mine, other, piece):
    return pl.pallas_call(
        pass_on_kernel,
        out_shape=jax.ShapeDtypeStruct((2 * BLOCK, piece.shape[1]), jnp.bfloat16),
        in_specs=[SM, SM, SM, pl.BlockSpec(memory_space=pl.ANY)],
        out_specs=VM,
        scratch_shapes=[pltpu.SemaphoreType.DMA((2,))],
        compiler_params=pltpu.CompilerParams(vmem_limit_bytes=1 << 20),
        name="pass_on",
    )(place, mine, other, piece)


def ring_pieces(x, place, lists, weights, qkv_weight):
    n, n_head = lax.axis_size("dom"), lax.axis_size("head")
    half = n // 4

    def send(v, by):
        return lax.ppermute(v, "dom", [(i, (i + by) % n) for i in range(n)])

    up, down = [x], [x]
    weight_t = qkv_weight.T
    mine = lists.reshape(n)
    swapped = mine.reshape(n // 2, 2)[:, ::-1].reshape(n)
    served = lax.all_to_all(
        jnp.stack([mine, swapped], axis=1), "dom", split_axis=0, concat_axis=0, tiled=True
    )
    both = jnp.concatenate(weights, axis=1)
    copied = jnp.broadcast_to(both[None], (n_head,) + both.shape)
    copied, served = lax.optimization_barrier((copied, served))
    ffn = lax.all_to_all(copied, "head", split_axis=0, concat_axis=0, tiled=True)
    ffn = ffn.reshape(-1, both.shape[1])
    for k in range(1, half):
        u_in, d_in = up[-1], down[-1]
        if k == 6:
            u_in, weight_t, above = lax.optimization_barrier((u_in, weight_t, above))
        up.append(send(u_in, 2))
        down.append(send(d_in, -2))
        if k == 4:
            up[-2], served = lax.optimization_barrier((up[-2], served))
            above = send(served, -2)
    u_in = pass_on(place, above[:, 0], above[:, 1], up[-1])
    u_in, ffn = lax.optimization_barrier((u_in, ffn))
    up.append(send(u_in, 2))
    return up[:half] + down[1:half] + up[half:], served, ffn, weight_t


def slot_of_entry(e, d, blocks, n):
    p = jnp.maximum(e - blocks, 0)
    core, z = d % 2, d // 2
    chips, half = n // 2, n // 4
    k = (z + chips - p // 2) % chips
    other = jnp.where((p % 2) == core, 0, chips)
    near = jnp.where(k < half, k, half - 1 + chips - k)
    near = jnp.where(k == half, chips - 1, near)
    return jnp.where(e < blocks, e, blocks + other + near)


def aggregate_kernel(place_ref, entry_ref, serve_ref, pattern_hbm, own_hbm, wt_hbm, *rest):
    pieces, (agg_ref, qkv_ref, table, wt_ref, pattern_ref, near_ref, sems, load_sems) = (
        rest[:-8], rest[-8:]
    )
    blocks, tiles = pattern_ref.shape[0], pattern_ref.shape[1]
    n_dom = serve_ref.shape[0]
    chips = n_dom // 2
    d = place_ref[0]
    pattern_load = pltpu.make_async_copy(pattern_hbm, pattern_ref, load_sems.at[0])
    own_load = pltpu.make_async_copy(own_hbm, table.at[pl.ds(0, blocks)], load_sems.at[1])
    wt_load = pltpu.make_async_copy(wt_hbm, wt_ref, load_sems.at[2])
    pattern_load.start()
    copies = start_copies(
        place_ref, serve_ref, 0, pieces[:-1], lambda slot: table.at[blocks + slot], sems
    )
    handed = pltpu.make_async_copy(
        pieces[-1], table.at[pl.ds(blocks + chips, chips)], sems.at[chips]
    )
    handed.start()
    own_load.start()
    wt_load.start()
    pattern_load.wait()

    def convert(b, carry):
        count = jnp.zeros((BLOCK, BLOCK), jnp.int32)
        for t in range(tiles):
            pattern = pattern_ref[b, t]
            count = count + pattern
            near_ref[b, :, t * BLOCK : (t + 1) * BLOCK] = pattern.astype(jnp.float32).astype(
                jnp.bfloat16
            )
        pattern_ref[b, 0] = count
        return carry

    lax.fori_loop(0, blocks, convert, 0)
    own_load.wait()
    for copy in copies + [handed]:
        copy.wait()

    def one_block(b, carry):
        acc = table[b].astype(jnp.float32)
        for t in range(0, tiles, 2):
            rows = [
                table[slot_of_entry(entry_ref[b, u], d, blocks, n_dom)] for u in (t, t + 1)
            ]
            acc = acc + jnp.dot(
                near_ref[b, :, t * BLOCK : (t + 2) * BLOCK],
                jnp.concatenate(rows, axis=0),
                preferred_element_type=jnp.float32,
            )
        degree = jnp.sum(pattern_ref[b, 0].astype(jnp.float32), axis=1, keepdims=True)
        span = pl.ds(pl.multiple_of(b * BLOCK, BLOCK), BLOCK)
        agg_ref[span, :] = (acc * lax.rsqrt(1.0 + degree)).astype(jnp.bfloat16)
        return carry

    lax.fori_loop(0, blocks, one_block, 0)
    wt_load.wait()
    third = qkv_ref.shape[0] // 3

    def one_third(i, carry):
        span = pl.ds(pl.multiple_of(i * third, third), third)
        qkv_ref[span, :] = lax.dot_general(
            wt_ref[span, :], agg_ref[...], (((1,), (1,)), ((), ())),
            preferred_element_type=jnp.float32,
        ).astype(jnp.bfloat16)
        return carry

    lax.fori_loop(0, 3, one_third, 0)


def aggregate(place, entries, serve, pattern, own, weight_t, pieces):
    rows, width = own.shape
    blocks, tiles = pattern.shape[0], pattern.shape[1]
    assert tiles % 2 == 0
    return pl.pallas_call(
        aggregate_kernel,
        out_shape=(
            jax.ShapeDtypeStruct((rows, width), jnp.bfloat16),
            jax.ShapeDtypeStruct((weight_t.shape[0], rows), jnp.bfloat16),
        ),
        in_specs=[SM, SM, SM] + [FAR] * (3 + len(pieces)),
        out_specs=(VM, VM),
        scratch_shapes=[
            pltpu.VMEM((blocks + serve.shape[0], BLOCK, width), jnp.bfloat16),
            pltpu.VMEM(weight_t.shape, jnp.bfloat16),
            pltpu.VMEM(pattern.shape, jnp.int32),
            pltpu.VMEM((blocks, BLOCK, tiles * BLOCK), jnp.bfloat16),
            pltpu.SemaphoreType.DMA((serve.shape[0] // 2 + 1,)),
            pltpu.SemaphoreType.DMA((3,)),
        ],
        name="aggregate",
    )(place, entries, serve, pattern, own.reshape(blocks, BLOCK, width), weight_t, *pieces)


def attend_kernel(key_ref, qkv_ref, out_ref, q_ref, kv_ref):
    sources, _, rows = qkv_ref.shape
    per = rows // BLOCK
    keys = key_ref.shape[1]

    def unpack(h, carry):
        for j in range(per):
            cols = slice(j * BLOCK, (j + 1) * BLOCK)
            q_ref[h * per + j] = qkv_ref[h, 0:HDIM, cols]
            kv_ref[h * per + j] = qkv_ref[h, HDIM : 3 * HDIM, cols]
        return carry

    lax.fori_loop(0, sources, unpack, 0)
    ones = jnp.ones((16, keys * BLOCK), jnp.bfloat16)

    def chosen(b, part):
        span = slice(part * HDIM, (part + 1) * HDIM)
        return jnp.concatenate([kv_ref[key_ref[b, k], span, :] for k in range(keys)], axis=1)

    def probabilities(scores):
        top = jnp.max(scores, axis=1, keepdims=True)
        return jnp.exp2((scores - top) * EXP2_SCALE).astype(jnp.bfloat16)

    def one_source(h, carry):
        ids = [h * per + j for j in range(per)]
        scores = [
            lax.dot_general(
                q_ref[b], chosen(b, 0), (((0,), (0,)), ((), ())),
                preferred_element_type=jnp.float32,
            )
            for b in ids
        ]
        values = [jnp.concatenate([chosen(b, 1), ones], axis=0) for b in ids]
        terms = [probabilities(s) for s in scores]
        for j in range(per):
            mixed = lax.dot_general(
                values[j], terms[j], (((1,), (1,)), ((), ())),
                preferred_element_type=jnp.float32,
            )
            mixed = mixed[0:HDIM] * (1.0 / mixed[HDIM : HDIM + 1])
            out_ref[h, :, j * BLOCK : (j + 1) * BLOCK] = mixed.astype(jnp.bfloat16)
        return carry

    lax.fori_loop(0, sources, one_source, 0)


def attend(key_blocks, qkv):
    sources, _, rows = qkv.shape
    blocks = sources * (rows // BLOCK)
    return pl.pallas_call(
        attend_kernel,
        out_shape=jax.ShapeDtypeStruct((sources, HDIM, rows), jnp.bfloat16),
        in_specs=[SM, VM],
        out_specs=VM,
        scratch_shapes=[
            pltpu.VMEM((blocks, HDIM, BLOCK), jnp.bfloat16),
            pltpu.VMEM((blocks, 2 * HDIM, BLOCK), jnp.bfloat16),
        ],
        compiler_params=pltpu.CompilerParams(vmem_limit_bytes=16 << 20),
        name="attend",
    )(key_blocks, qkv)


def finish_kernel(context_ref, agg_ref, attn_ref, gain_ref, ffn_ref, out_ref, normed_ref, total_ref):
    _, width = agg_ref.shape
    hidden_units = ffn_ref.shape[0]
    mixed = agg_ref[...].astype(jnp.float32) + jnp.dot(
        context_ref[...].T, attn_ref[...], preferred_element_type=jnp.float32
    )
    mean_square = jnp.mean(mixed * mixed, axis=1, keepdims=True)
    normed = (mixed * lax.rsqrt(mean_square + 1e-06) * gain_ref[...]).astype(jnp.bfloat16)
    normed_ref[...] = normed
    total_ref[...] = normed.astype(jnp.float32)
    chunk = 512

    def one_chunk(c, carry):
        span = pl.ds(pl.multiple_of(c * chunk, chunk), chunk)
        hidden = lax.dot_general(
            normed_ref[...], ffn_ref[span, 0:width], (((1,), (1,)), ((), ())),
            preferred_element_type=jnp.float32,
        )
        hidden = jax.nn.gelu(hidden).astype(jnp.bfloat16)
        total_ref[...] += jnp.dot(
            hidden, ffn_ref[span, width : 2 * width], preferred_element_type=jnp.float32
        )
        return carry

    lax.fori_loop(0, hidden_units // chunk, one_chunk, 0)
    out_ref[...] = total_ref[...].astype(jnp.bfloat16)


def finish(context_t, agg, attn_weight, gain, ffn):
    rows, width = agg.shape
    return pl.pallas_call(
        finish_kernel,
        out_shape=jax.ShapeDtypeStruct((rows, width), jnp.bfloat16),
        in_specs=[VM] * 5,
        out_specs=VM,
        scratch_shapes=[
            pltpu.VMEM((rows, width), jnp.bfloat16),
            pltpu.VMEM((rows, width), jnp.float32),
        ],
        compiler_params=pltpu.CompilerParams(vmem_limit_bytes=20 << 20),
        name="finish",
    )(context_t, agg, attn_weight, gain, ffn)


def shards(
    features,
    tile_pattern,
    tile_source,
    serve_list,
    key_blocks,
    qkv_weight,
    attn_weight,
    norm_gain,
    expand_weight,
    reduce_weight,
):
    n_head = lax.axis_size("head")
    width = features.shape[1]
    rows = features.shape[0]

    place = lax.axis_index("dom").reshape(1)
    n_dom = lax.axis_size("dom")
    pieces, served, ffn, weight_t = ring_pieces(
        features, place, serve_list, (expand_weight, reduce_weight), qkv_weight
    )
    handed = lax.ppermute(
        pick(place, served[:, 1], pieces), "dom", [(i, i ^ 1) for i in range(n_dom)]
    )
    agg, qkv_t = aggregate(
        place, tile_source, served[:, 0], tile_pattern, features, weight_t, pieces + [handed]
    )
    qkv = lax.all_to_all(
        qkv_t.reshape(n_head, 3 * HDIM, rows), "head", split_axis=0, concat_axis=0, tiled=True
    )
    context = attend(key_blocks, qkv)
    context_t = lax.all_to_all(
        context, "head", split_axis=0, concat_axis=0, tiled=True
    ).reshape(HEADS * HDIM, rows)
    return finish(context_t, agg, attn_weight, norm_gain.reshape(1, width), ffn)


def solution(mesh):
    placed = (
        P(("dom", "head"), None),
        P(("dom", "head"), None, None, None),
        P(("dom", "head"), None),
        P("dom", "head", None, None),
        P("dom", None),
        P(),
        P(),
        P(),
        P("head", None),
        P("head", None),
    )

    return jax.shard_map(
        shards, mesh=mesh, in_specs=placed, out_specs=P(("dom", "head"), None), check_vma=False
    )
```

```python
import math

import jax
import jax.numpy as jnp
from jax import lax
from jax.experimental import pallas as pl
from jax.experimental.pallas import tpu as pltpu
from jax.sharding import PartitionSpec as P


HEADS = 16
HDIM = 32
BLOCK = 128
VM = pl.BlockSpec(memory_space=pltpu.VMEM)
SM = pl.BlockSpec(memory_space=pltpu.SMEM)
FAR = pl.BlockSpec(memory_space=pltpu.HBM)
EXP2_SCALE = math.log2(math.e) / math.sqrt(HDIM)


def start_copies(place_ref, wanted_ref, far_row, pieces, slot_of, sems):
    n = wanted_ref.shape[0]
    core, z = place_ref[0] % 2, place_ref[0] // 2
    chips, half = n // 2, n // 4
    copies = []
    steps = list(range(half)) + [chips - k for k in range(1, half)] + [half]
    for slot, (piece, step) in enumerate(zip(pieces, steps)):
        block = wanted_ref[2 * ((z + chips - step) % chips) + core]
        if step == half:
            block = far_row
        rows = pl.ds(pl.multiple_of(block * BLOCK, BLOCK), BLOCK)
        copies.append(pltpu.make_async_copy(piece.at[rows, :], slot_of(slot), sems.at[slot]))
        copies[-1].start()
    return copies


def pick_kernel(place_ref, wanted_ref, *refs):
    pieces, (out_ref, sems) = refs[:-2], refs[-2:]
    for copy in start_copies(
        place_ref, wanted_ref, 0, pieces, lambda slot: out_ref.at[slot], sems
    ):
        copy.wait()


def pick(place, wanted, pieces):
    return pl.pallas_call(
        pick_kernel,
        out_shape=jax.ShapeDtypeStruct((len(pieces), BLOCK, pieces[0].shape[1]), jnp.bfloat16),
        in_specs=[SM, SM] + [FAR] * len(pieces),
        out_specs=VM,
        scratch_shapes=[pltpu.SemaphoreType.DMA((len(pieces),))],
        name="pick",
    )(place, wanted, *pieces)


def pass_on_kernel(place_ref, mine_ref, other_ref, piece, out_ref, sems):
    n = mine_ref.shape[0]
    core, z = place_ref[0] % 2, place_ref[0] // 2
    chips, half = n // 2, n // 4
    source = 2 * ((z + chips - (half - 1)) % chips) + core
    copies = []
    for i, ref in enumerate((mine_ref, other_ref)):
        rows = pl.ds(pl.multiple_of(ref[source] * BLOCK, BLOCK), BLOCK)
        copies.append(
            pltpu.make_async_copy(
                piece.at[rows, :], out_ref.at[pl.ds(i * BLOCK, BLOCK), :], sems.at[i]
            )
        )
        copies[-1].start()
    for copy in copies:
        copy.wait()


def pass_on(place, mine, other, piece):
    return pl.pallas_call(
        pass_on_kernel,
        out_shape=jax.ShapeDtypeStruct((2 * BLOCK, piece.shape[1]), jnp.bfloat16),
        in_specs=[SM, SM, SM, pl.BlockSpec(memory_space=pl.ANY)],
        out_specs=VM,
        scratch_shapes=[pltpu.SemaphoreType.DMA((2,))],
        compiler_params=pltpu.CompilerParams(vmem_limit_bytes=1 << 20),
        name="pass_on",
    )(place, mine, other, piece)


def ring_pieces(x, place, lists, weights, qkv_weight):
    n, n_head = lax.axis_size("dom"), lax.axis_size("head")
    half = n // 4

    def send(v, by):
        return lax.ppermute(v, "dom", [(i, (i + by) % n) for i in range(n)])

    up, down = [x], [x]
    weight_t = qkv_weight.T
    mine = lists.reshape(n)
    swapped = mine.reshape(n // 2, 2)[:, ::-1].reshape(n)
    served = lax.all_to_all(
        jnp.stack([mine, swapped], axis=1), "dom", split_axis=0, concat_axis=0, tiled=True
    )
    both = jnp.concatenate(weights, axis=1)
    copied = jnp.broadcast_to(both[None], (n_head,) + both.shape)
    copied, served = lax.optimization_barrier((copied, served))
    ffn = lax.all_to_all(copied, "head", split_axis=0, concat_axis=0, tiled=True)
    ffn = ffn.reshape(-1, both.shape[1])
    for k in range(1, half):
        u_in, d_in = up[-1], down[-1]
        if k == 6:
            u_in, weight_t = lax.optimization_barrier((u_in, weight_t))
        if k == 7:
            d_in, above = lax.optimization_barrier((d_in, above))
        up.append(send(u_in, 2))
        down.append(send(d_in, -2))
        if k == 4:
            up[-2], served = lax.optimization_barrier((up[-2], served))
            above = send(served, -2)
    u_in = pass_on(place, above[:, 0], above[:, 1], up[-1])
    u_in, ffn = lax.optimization_barrier((u_in, ffn))
    up.append(send(u_in, 2))
    return up[:half] + down[1:half] + up[half:], served, ffn, weight_t


def slot_of_entry(e, d, blocks, n):
    p = jnp.maximum(e - blocks, 0)
    core, z = d % 2, d // 2
    chips, half = n // 2, n // 4
    k = (z + chips - p // 2) % chips
    other = jnp.where((p % 2) == core, 0, chips)
    near = jnp.where(k < half, k, half - 1 + chips - k)
    near = jnp.where(k == half, chips - 1, near)
    return jnp.where(e < blocks, e, blocks + other + near)


def aggregate_kernel(place_ref, entry_ref, serve_ref, pattern_hbm, own_hbm, wt_hbm, *rest):
    pieces, (agg_ref, qkv_ref, table, wt_ref, pattern_ref, near_ref, sems, load_sems) = (
        rest[:-8], rest[-8:]
    )
    blocks, tiles = pattern_ref.shape[0], pattern_ref.shape[1]
    n_dom = serve_ref.shape[0]
    chips = n_dom // 2
    d = place_ref[0]
    pattern_load = pltpu.make_async_copy(pattern_hbm, pattern_ref, load_sems.at[0])
    own_load = pltpu.make_async_copy(own_hbm, table.at[pl.ds(0, blocks)], load_sems.at[1])
    wt_load = pltpu.make_async_copy(wt_hbm, wt_ref, load_sems.at[2])
    pattern_load.start()
    copies = start_copies(
        place_ref, serve_ref, 0, pieces[:-2], lambda slot: table.at[blocks + slot], sems
    )
    other = blocks + chips
    copies.append(
        pltpu.make_async_copy(
            pieces[-2], table.at[pl.ds(other, chips - 1)], sems.at[chips]
        )
    )
    copies.append(
        pltpu.make_async_copy(pieces[-1], table.at[other + chips - 1], sems.at[chips + 1])
    )
    copies[-2].start()
    copies[-1].start()
    own_load.start()
    wt_load.start()
    pattern_load.wait()

    def convert(b, carry):
        count = jnp.zeros((BLOCK, BLOCK), jnp.int32)
        for t in range(tiles):
            pattern = pattern_ref[b, t]
            count = count + pattern
            near_ref[b, :, t * BLOCK : (t + 1) * BLOCK] = pattern.astype(jnp.float32).astype(
                jnp.bfloat16
            )
        pattern_ref[b, 0] = count
        return carry

    lax.fori_loop(0, blocks, convert, 0, unroll=True)
    own_load.wait()
    for copy in copies:
        copy.wait()

    def one_block(b, carry):
        acc = table[b].astype(jnp.float32)
        for t in range(0, tiles, 2):
            rows = [
                table[slot_of_entry(entry_ref[b, u], d, blocks, n_dom)] for u in (t, t + 1)
            ]
            acc = acc + jnp.dot(
                near_ref[b, :, t * BLOCK : (t + 2) * BLOCK],
                jnp.concatenate(rows, axis=0),
                preferred_element_type=jnp.float32,
            )
        degree = jnp.sum(pattern_ref[b, 0].astype(jnp.float32), axis=1, keepdims=True)
        span = pl.ds(pl.multiple_of(b * BLOCK, BLOCK), BLOCK)
        agg_ref[span, :] = (acc * lax.rsqrt(1.0 + degree)).astype(jnp.bfloat16)
        return carry

    lax.fori_loop(0, blocks, one_block, 0, unroll=True)
    wt_load.wait()
    third = qkv_ref.shape[0] // 3

    def one_third(i, carry):
        span = pl.ds(pl.multiple_of(i * third, third), third)
        qkv_ref[span, :] = lax.dot_general(
            wt_ref[span, :], agg_ref[...], (((1,), (1,)), ((), ())),
            preferred_element_type=jnp.float32,
        ).astype(jnp.bfloat16)
        return carry

    lax.fori_loop(0, 3, one_third, 0)


def aggregate(place, entries, serve, pattern, own, weight_t, pieces):
    rows, width = own.shape
    blocks, tiles = pattern.shape[0], pattern.shape[1]
    assert tiles % 2 == 0
    return pl.pallas_call(
        aggregate_kernel,
        out_shape=(
            jax.ShapeDtypeStruct((rows, width), jnp.bfloat16),
            jax.ShapeDtypeStruct((weight_t.shape[0], rows), jnp.bfloat16),
        ),
        in_specs=[SM, SM, SM] + [FAR] * (3 + len(pieces)),
        out_specs=(VM, VM),
        scratch_shapes=[
            pltpu.VMEM((blocks + serve.shape[0], BLOCK, width), jnp.bfloat16),
            pltpu.VMEM(weight_t.shape, jnp.bfloat16),
            pltpu.VMEM(pattern.shape, jnp.int32),
            pltpu.VMEM((blocks, BLOCK, tiles * BLOCK), jnp.bfloat16),
            pltpu.SemaphoreType.DMA((serve.shape[0] // 2 + 2,)),
            pltpu.SemaphoreType.DMA((3,)),
        ],
        name="aggregate",
    )(place, entries, serve, pattern, own.reshape(blocks, BLOCK, width), weight_t, *pieces)


def attend_kernel(key_ref, qkv_ref, out_ref, q_ref, kv_ref):
    sources, _, rows = qkv_ref.shape
    per = rows // BLOCK
    keys = key_ref.shape[1]

    def unpack(h, carry):
        for j in range(per):
            cols = slice(j * BLOCK, (j + 1) * BLOCK)
            q_ref[h * per + j] = qkv_ref[h, 0:HDIM, cols]
            kv_ref[h * per + j] = qkv_ref[h, HDIM : 3 * HDIM, cols]
        return carry

    lax.fori_loop(0, sources, unpack, 0)
    ones = jnp.ones((16, keys * BLOCK), jnp.bfloat16)

    def chosen(b, part):
        span = slice(part * HDIM, (part + 1) * HDIM)
        return jnp.concatenate([kv_ref[key_ref[b, k], span, :] for k in range(keys)], axis=1)

    def probabilities(scores):
        top = jnp.max(scores, axis=1, keepdims=True)
        return jnp.exp2((scores - top) * EXP2_SCALE).astype(jnp.bfloat16)

    def one_source(h, carry):
        ids = [h * per + j for j in range(per)]
        scores = [
            lax.dot_general(
                q_ref[b], chosen(b, 0), (((0,), (0,)), ((), ())),
                preferred_element_type=jnp.float32,
            )
            for b in ids
        ]
        values = [jnp.concatenate([chosen(b, 1), ones], axis=0) for b in ids]
        terms = [probabilities(s) for s in scores]
        for j in range(per):
            mixed = lax.dot_general(
                values[j], terms[j], (((1,), (1,)), ((), ())),
                preferred_element_type=jnp.float32,
            )
            mixed = mixed[0:HDIM] * (1.0 / mixed[HDIM : HDIM + 1])
            out_ref[h, :, j * BLOCK : (j + 1) * BLOCK] = mixed.astype(jnp.bfloat16)
        return carry

    lax.fori_loop(0, sources, one_source, 0)


def attend(key_blocks, qkv):
    sources, _, rows = qkv.shape
    blocks = sources * (rows // BLOCK)
    return pl.pallas_call(
        attend_kernel,
        out_shape=jax.ShapeDtypeStruct((sources, HDIM, rows), jnp.bfloat16),
        in_specs=[SM, VM],
        out_specs=VM,
        scratch_shapes=[
            pltpu.VMEM((blocks, HDIM, BLOCK), jnp.bfloat16),
            pltpu.VMEM((blocks, 2 * HDIM, BLOCK), jnp.bfloat16),
        ],
        compiler_params=pltpu.CompilerParams(vmem_limit_bytes=16 << 20),
        name="attend",
    )(key_blocks, qkv)


def finish_kernel(
    context_ref, agg_ref, attn_ref, gain_ref, ffn_hbm, out_ref, normed_ref, total_ref, ffn_ref, sems
):
    _, width = agg_ref.shape
    hidden_units = ffn_ref.shape[0]
    chunk = hidden_units // sems.shape[0]
    loads = []
    for c in range(sems.shape[0]):
        span = pl.ds(c * chunk, chunk)
        loads.append(pltpu.make_async_copy(ffn_hbm.at[span, :], ffn_ref.at[span, :], sems.at[c]))
        loads[-1].start()
    mixed = agg_ref[...].astype(jnp.float32) + jnp.dot(
        context_ref[...].T, attn_ref[...], preferred_element_type=jnp.float32
    )
    mean_square = jnp.mean(mixed * mixed, axis=1, keepdims=True)
    normed = (mixed * lax.rsqrt(mean_square + 1e-06) * gain_ref[...]).astype(jnp.bfloat16)
    normed_ref[...] = normed
    total_ref[...] = normed.astype(jnp.float32)
    for c, load in enumerate(loads):
        load.wait()
        span = slice(c * chunk, (c + 1) * chunk)
        hidden = lax.dot_general(
            normed_ref[...], ffn_ref[span, 0:width], (((1,), (1,)), ((), ())),
            preferred_element_type=jnp.float32,
        )
        hidden = jax.nn.gelu(hidden).astype(jnp.bfloat16)
        total_ref[...] += jnp.dot(
            hidden, ffn_ref[span, width : 2 * width], preferred_element_type=jnp.float32
        )
    out_ref[...] = total_ref[...].astype(jnp.bfloat16)


def finish(context_t, agg, attn_weight, gain, ffn):
    rows, width = agg.shape
    return pl.pallas_call(
        finish_kernel,
        out_shape=jax.ShapeDtypeStruct((rows, width), jnp.bfloat16),
        in_specs=[VM] * 4 + [FAR],
        out_specs=VM,
        scratch_shapes=[
            pltpu.VMEM((rows, width), jnp.bfloat16),
            pltpu.VMEM((rows, width), jnp.float32),
            pltpu.VMEM(ffn.shape, jnp.bfloat16),
            pltpu.SemaphoreType.DMA((4,)),
        ],
        compiler_params=pltpu.CompilerParams(vmem_limit_bytes=24 << 20),
        name="finish",
    )(context_t, agg, attn_weight, gain, ffn)


def shards(
    features,
    tile_pattern,
    tile_source,
    serve_list,
    key_blocks,
    qkv_weight,
    attn_weight,
    norm_gain,
    expand_weight,
    reduce_weight,
):
    n_head = lax.axis_size("head")
    width = features.shape[1]
    rows = features.shape[0]

    place = lax.axis_index("dom").reshape(1)
    n_dom = lax.axis_size("dom")
    pieces, served, ffn, weight_t = ring_pieces(
        features, place, serve_list, (expand_weight, reduce_weight), qkv_weight
    )
    swap = [(i, i ^ 1) for i in range(n_dom)]
    chosen = pick(place, served[:, 1], pieces[:-1])
    handed = lax.ppermute(chosen, "dom", swap)
    handed_last = lax.ppermute(pieces[-1][BLOCK:], "dom", swap)
    agg, qkv_t = aggregate(
        place, tile_source, served[:, 0], tile_pattern, features, weight_t,
        pieces + [handed, handed_last],
    )
    qkv = lax.all_to_all(
        qkv_t.reshape(n_head, 3 * HDIM, rows), "head", split_axis=0, concat_axis=0, tiled=True
    )
    context = attend(key_blocks, qkv)
    context_t = lax.all_to_all(
        context, "head", split_axis=0, concat_axis=0, tiled=True
    ).reshape(HEADS * HDIM, rows)
    return finish(context_t, agg, attn_weight, norm_gain.reshape(1, width), ffn)


def solution(mesh):
    placed = (
        P(("dom", "head"), None),
        P(("dom", "head"), None, None, None),
        P(("dom", "head"), None),
        P("dom", "head", None, None),
        P("dom", None),
        P(),
        P(),
        P(),
        P("head", None),
        P("head", None),
    )

    return jax.shard_map(
        shards, mesh=mesh, in_specs=placed, out_specs=P(("dom", "head"), None), check_vma=False
    )
```
